32 devices in a mesh: dp: 8 (over z, core), seq: 4 (over y, x).
Axes of the slice: x: 2, y: 2, z: 4, core: 2. Of those that a mesh axis runs over, the one named last changes fastest.
Arguments:
- hidden_in: float32 [8, 512, 1024], P('dp', 'seq'), may hold values from -6 to 6
- segments: int32 [8, 512], P('dp', 'seq'), may hold values from 0 to 3, as said below
- positions: int32 [8, 512], P('dp', 'seq'), may hold values from 0 to 383, as said below
- project_weight: bfloat16 [1024, 3072], P(('dp', 'seq'))
- project_bias: bfloat16 [3072], P(('dp', 'seq')), may hold values from -3 to 3
- dense_weight: bfloat16 [1024, 1024], P(('dp', 'seq')), may hold values from -1.5 to 1.5
- dense_bias: bfloat16 [1024], P(('dp', 'seq')), may hold values from -3 to 3
- expand_weight: bfloat16 [1024, 4096], P(('dp', 'seq')), may hold values from -0.1875 to 0.1875
- expand_bias: bfloat16 [4096], P(('dp', 'seq')), may hold values from -3 to 3
- shrink_weight: bfloat16 [4096, 1024], P(('dp', 'seq')), may hold values from -0.09375 to 0.09375
- shrink_bias: bfloat16 [1024], P(('dp', 'seq')), may hold values from -3 to 3
- first_gain: bfloat16 [1024], P(('dp', 'seq')), may hold values from 0.5 to 1.5
- first_shift: bfloat16 [1024], P(('dp', 'seq')), may hold values from -3 to 3
- second_gain: bfloat16 [1024], P(('dp', 'seq')), may hold values from 0.5 to 1.5
- second_shift: bfloat16 [1024], P(('dp', 'seq')), may hold values from -3 to 3
- cotangent: float32 [8, 512, 1024], P('dp', 'seq'), may hold values from -6 to 6
Outputs:
- layer_out: float32 [8, 512, 1024], P('dp', 'seq')
- grad_input: float32 [8, 512, 1024], P('dp', 'seq')
- grad_project_weight: float32 [1024, 3072], P(('dp', 'seq'))
- grad_project_bias: float32 [3072], P(('dp', 'seq'))
- grad_dense_weight: float32 [1024, 1024], P(('dp', 'seq'))
- grad_dense_bias: float32 [1024], P(('dp', 'seq'))
- grad_expand_weight: float32 [1024, 4096], P(('dp', 'seq'))
- grad_expand_bias: float32 [4096], P(('dp', 'seq'))
- grad_shrink_weight: float32 [4096, 1024], P(('dp', 'seq'))
- grad_shrink_bias: float32 [1024], P(('dp', 'seq'))
- grad_first_gain: float32 [1024], P(('dp', 'seq'))
- grad_first_shift: float32 [1024], P(('dp', 'seq'))
- grad_second_gain: float32 [1024], P(('dp', 'seq'))
- grad_second_shift: float32 [1024], P(('dp', 'seq'))
The draws below stay inside these ranges and needn't reach their ends.
Inputs may be any that keep to these rules, and one draw needn't show every extreme that they name: `segments`: along a sequence the numbers never fall; every sequence holds exactly 4 documents of 32 or more tokens, one of exactly 384 tokens. `positions`: A token's offset from the first token of its document.
All inputs are finite; a program needn't handle non-finite values.
Results may differ from the reference program's by a relative error of at most 0.011.
Values may be sent and summed in bfloat16 or wider, within the bound.
No kernel may reach another device: no remote copies, remote signals or barrier semaphores. Data moves between devices by JAX's collectives and lax.ppermute only.
A program may use at most 256 MiB of HBM per device.

```python
import math
import jax
import jax.numpy as jnp
from jax import lax

D = 1024
HEADS = 16
HEAD_DIM = 64
ROT = 16
FF = 4096
DOCS = 4
LEN = 512
SEQS = 8
DOC_MOST = 384
DOC_LEAST = 32


def documents(key):
    base = jax.random.fold_in(key, 11)
    first_key, second_key = jax.random.split(base)
    spare = LEN - DOC_MOST - (DOCS - 1) * DOC_LEAST
    weights = jax.random.randint(first_key, (SEQS, DOCS - 1), 1, 64)
    extra = weights * spare // jnp.sum(weights, axis=1, keepdims=True)
    missing = spare - jnp.sum(extra, axis=1, keepdims=True)
    extra = extra + jnp.concatenate([jnp.zeros((SEQS, DOCS - 2), jnp.int32), missing], 1)
    lengths = jnp.concatenate([jnp.full((SEQS, 1), DOC_MOST, jnp.int32), DOC_LEAST + extra], 1)
    orders = jax.vmap(lambda row_key: jax.random.permutation(row_key, DOCS))(jax.random.split(second_key, SEQS))
    lengths = jnp.take_along_axis(lengths, orders, 1)
    ends = jnp.cumsum(lengths, 1)
    starts = ends - lengths
    index = jnp.arange(LEN, dtype=jnp.int32)
    segment = jnp.sum((index[None, :, None] >= ends[:, None, :]).astype(jnp.int32), 2).astype(jnp.int32)
    offset = index[None, :] - jnp.take_along_axis(starts, segment, 1)
    return (segment.astype(jnp.int32), offset.astype(jnp.int32))


def draw_segments(key, part):
    return documents(key)[0]


def draw_positions(key, part):
    return documents(key)[1]


def draw_project_weight(key, part):
    base = jax.random.fold_in(key, 23)
    first_key = jax.random.fold_in(base, 0)
    weight = jax.random.normal(first_key, (D, 3 * D), jnp.float32) * D ** (-0.5)
    return weight.astype(jnp.bfloat16)


def strengthened(entries, own_key, source, target, shards_of, factor):
    owner, partner = [(jnp.arange(entries.shape[axis_at]) // (entries.shape[axis_at] // shards_of)).reshape([-1 if axis == axis_at else 1 for axis in range(entries.ndim)]) for axis_at in (source, target)]
    chosen = jax.random.permutation(own_key, shards_of)[partner]
    strong = (owner == chosen) | (owner == (partner + shards_of // 2) % shards_of)
    return jnp.where(strong, factor * entries, entries)


def level_of(stream_key, shape, cuts, low, top_value):
    loudness = 1.0
    for position, blocks in cuts:
        steps = jax.random.uniform(jax.random.fold_in(jax.random.fold_in(stream_key, 6), position), (blocks,), jnp.float32, low / len(cuts), top_value / len(cuts))
        loudness = loudness * jnp.repeat(jnp.exp(steps), shape[position] // blocks).reshape((-1,) + (1,) * (len(shape) - 1 - position))
    return loudness


def centred(key, extent, deviation, bound, cuts=(), kind=jnp.bfloat16):
    values = deviation * jax.random.normal(key, extent, jnp.float32)
    if cuts:
        values = values * level_of(key, extent, cuts, -0.22, 0.18)
    return jnp.clip(values, -bound, bound).astype(kind)


def noise_with(key, shape, scale, reach, cuts, heavy, kind=jnp.bfloat16):
    result = scale * jax.random.normal(key, shape, jnp.float32)
    if cuts:
        result = result * level_of(key, shape, cuts, -0.22, 0.18)
    return jnp.clip(strengthened(result, jax.random.fold_in(key, 3), *heavy), -reach, reach).astype(kind)


def setup_inputs(seed: int = 0) -> dict:
    streams_of = jax.random.split(jax.random.key(seed), 17)
    return {
        "hidden_in": centred(streams_of[0], (SEQS, LEN, D), 1.0, 6.0, ((0, 8), (1, 4)), jnp.float32),
        "segments": draw_segments(jax.random.fold_in(streams_of[16], 71), 0),
        "positions": draw_positions(jax.random.fold_in(streams_of[16], 71), 0),
        "project_weight": draw_project_weight(jax.random.fold_in(streams_of[16], 71), 0),
        "project_bias": centred(streams_of[4], (3 * D,), 0.5, 3.0, ((0, 32),)),
        "dense_weight": centred(streams_of[5], (D, D), (D // 64) ** -0.5, 1.5, ((0, 32),)),
        "dense_bias": centred(streams_of[6], (D,), 0.5, 3.0, ((0, 32),)),
        "expand_weight": centred(streams_of[7], (D, FF), D ** -0.5, 0.1875, ((0, 32),)),
        "expand_bias": centred(streams_of[8], (FF,), 0.5, 3.0, ((0, 32),)),
        "shrink_weight": centred(streams_of[9], (FF, D), FF ** -0.5, 0.09375, ((0, 32),)),
        "shrink_bias": centred(streams_of[10], (D,), 0.5, 3.0, ((0, 32),)),
        "first_gain": jnp.clip(1.0 + 0.1 * jax.random.normal(streams_of[11], (D,), jnp.float32), 0.5, 1.5).astype(jnp.bfloat16),
        "first_shift": centred(streams_of[12], (D,), 0.5, 3.0, ((0, 32),)),
        "second_gain": jnp.clip(1.0 + 0.1 * jax.random.normal(streams_of[13], (D,), jnp.float32), 0.5, 1.5).astype(jnp.bfloat16),
        "second_shift": centred(streams_of[14], (D,), 0.5, 3.0, ((0, 32),)),
        "cotangent": noise_with(streams_of[15], (SEQS, LEN, D), 1.0, 6.0, ((0, 8), (1, 4)), (1, 2, 4, 2.0), jnp.float32),
    }


EPS = 1e-05

def normalize(values):
    centre = lax.optimization_barrier(jnp.mean(values, axis=-1, keepdims=True))
    shifted = values - centre
    inv_std = lax.rsqrt(lax.optimization_barrier(jnp.mean(shifted * shifted, axis=-1, keepdims=True)) + EPS)
    return (shifted * inv_std, inv_std)

def rotary_tables(offsets):
    half = ROT // 2
    inverse = jnp.exp(jnp.arange(half, dtype=jnp.float32) * (-2.0 * math.log(10000.0) / ROT))
    angles = offsets.astype(jnp.float32)[:, None] * inverse[None, :]
    return (jnp.concatenate([jnp.cos(angles), jnp.cos(angles)], 1), jnp.concatenate([jnp.sin(angles), jnp.sin(angles)], 1))

def rotate(values, cosine, sine):
    half = ROT // 2
    front = values[..., :ROT]
    turned = jnp.concatenate([-front[..., half:], front[..., :half]], -1)
    return jnp.concatenate([front * cosine[:, None, :] + turned * sine[:, None, :], values[..., ROT:]], -1)

def rotate_back(grad, cosine, sine):
    half = ROT // 2
    front = grad[..., :ROT]
    scaled = front * sine[:, None, :]
    turned = jnp.concatenate([scaled[..., half:], -scaled[..., :half]], -1)
    return jnp.concatenate([front * cosine[:, None, :] + turned, grad[..., ROT:]], -1)

def gelu_slope(pre):
    cdf = 0.5 * (1.0 + jax.scipy.special.erf(pre * (1.0 / math.sqrt(2.0))))
    return cdf + pre * jnp.exp(-0.5 * pre * pre) * (1.0 / math.sqrt(2.0 * math.pi))

def contract_rows(left, right):
    return lax.dot_general(left, right, (((0,), (0,)), ((), ())), preferred_element_type=jnp.float32)

def contract_cols(left, right):
    return lax.dot_general(left, right, (((1,), (1,)), ((), ())), preferred_element_type=jnp.float32)

def attend(queries, keys, values, allowed):
    scale = 1.0 / math.sqrt(HEAD_DIM)

    def one_head(carry, parts):
        query, key, value = parts
        scores = jnp.where(allowed, contract_cols(query, key) * scale, -1e+30)
        top = lax.optimization_barrier(jnp.max(scores, -1, keepdims=True))
        total = lax.optimization_barrier(jnp.sum(jnp.where(allowed, jnp.exp(scores - top), 0.0), -1, keepdims=True))
        log_total = top + jnp.log(total)
        probs = jnp.where(allowed, jnp.exp(scores - log_total), 0.0).astype(jnp.bfloat16)
        return (carry, (jnp.dot(probs, value, preferred_element_type=jnp.float32), log_total[:, 0]))
    unused, outputs = lax.scan(one_head, None, (queries, keys, values))
    return outputs

def attend_back(queries, keys, values, allowed, log_total, grad_heads, row_dots):
    scale = 1.0 / math.sqrt(HEAD_DIM)

    def one_head(carry, parts):
        query, key, value, head_total, grad_head, head_dots = parts
        scores = jnp.where(allowed, contract_cols(query, key) * scale, -1e+30)
        probs = jnp.where(allowed, jnp.exp(scores - head_total[:, None]), 0.0)
        probs_low = probs.astype(jnp.bfloat16)
        grad_probs = contract_cols(grad_head, value)
        grad_scores = (probs * (grad_probs - head_dots[:, None]) * scale).astype(jnp.bfloat16)
        grad_query = jnp.dot(grad_scores, key, preferred_element_type=jnp.float32)
        grad_key = contract_rows(grad_scores, query)
        grad_value = contract_rows(probs_low, grad_head)
        return (carry, (grad_query, grad_key, grad_value))
    unused, outputs = lax.scan(one_head, None, (queries, keys, values, log_total, grad_heads, row_dots))
    return outputs

def one_sequence(params, tokens, seg_row, pos_row, grad_top):
    project_weight, project_bias, dense_weight, dense_bias, expand_weight, expand_bias, shrink_weight, shrink_bias, first_gain, first_shift, second_gain, second_shift = params
    count = tokens.shape[0]
    gain_one = first_gain.astype(jnp.float32)
    gain_two = second_gain.astype(jnp.float32)
    normed, inv_std = normalize(tokens)
    first_in = (normed * gain_one + first_shift.astype(jnp.float32)).astype(jnp.bfloat16)
    proj = jnp.dot(first_in, project_weight, preferred_element_type=jnp.float32) + project_bias.astype(jnp.float32)
    cosine, sine = rotary_tables(pos_row)
    query = rotate(proj[:, :D].reshape(count, HEADS, HEAD_DIM), cosine, sine).astype(jnp.bfloat16)
    key_all = rotate(proj[:, D:2 * D].reshape(count, HEADS, HEAD_DIM), cosine, sine).astype(jnp.bfloat16)
    value_all = proj[:, 2 * D:].astype(jnp.bfloat16)
    index = jnp.arange(count)
    allowed = (index[None, :] <= index[:, None]) & (seg_row[None, :] == seg_row[:, None])
    query_heads = query.transpose(1, 0, 2)
    key_heads = key_all.transpose(1, 0, 2)
    value_heads = value_all.reshape(count, HEADS, HEAD_DIM).transpose(1, 0, 2)
    mixed, log_total = attend(query_heads, key_heads, value_heads, allowed)
    mixed_low = mixed.astype(jnp.bfloat16)
    mixed_flat = mixed_low.transpose(1, 0, 2).reshape(count, D)
    attn_out = jnp.dot(mixed_flat, dense_weight, preferred_element_type=jnp.float32) + dense_bias.astype(jnp.float32)
    second_in = (normed * gain_two + second_shift.astype(jnp.float32)).astype(jnp.bfloat16)
    pre = jnp.dot(second_in, expand_weight, preferred_element_type=jnp.float32) + expand_bias.astype(jnp.float32)
    act = jax.nn.gelu(pre, approximate=False).astype(jnp.bfloat16)
    mlp_out = jnp.dot(act, shrink_weight, preferred_element_type=jnp.float32) + shrink_bias.astype(jnp.float32)
    layer_out = tokens + attn_out + mlp_out
    grad_low = grad_top.astype(jnp.bfloat16)
    bias_sum = lax.optimization_barrier(jnp.sum(grad_top, 0))
    grad_pre = contract_cols(grad_low, shrink_weight) * gelu_slope(pre)
    grad_pre_low = grad_pre.astype(jnp.bfloat16)
    grad_second = contract_cols(grad_pre_low, expand_weight)
    grad_mixed = contract_cols(grad_low, dense_weight).astype(jnp.bfloat16)
    grad_heads = grad_mixed.reshape(count, HEADS, HEAD_DIM).transpose(1, 0, 2)
    row_dots = lax.optimization_barrier(jnp.sum(grad_heads.astype(jnp.float32) * mixed_low.astype(jnp.float32), -1))
    grad_query, grad_key, grad_value = attend_back(query_heads, key_heads, value_heads, allowed, log_total, grad_heads, row_dots)
    grad_proj = jnp.concatenate([rotate_back(grad_query.transpose(1, 0, 2), cosine, sine).reshape(count, D), rotate_back(grad_key.transpose(1, 0, 2), cosine, sine).reshape(count, D), grad_value.transpose(1, 0, 2).reshape(count, D)], 1)
    grad_proj_low = grad_proj.astype(jnp.bfloat16)
    grad_first = contract_cols(grad_proj_low, project_weight)
    grad_normed = grad_first * gain_one + grad_second * gain_two
    grad_input = grad_top + inv_std * (grad_normed - lax.optimization_barrier(jnp.mean(grad_normed, -1, keepdims=True)) - normed * lax.optimization_barrier(jnp.mean(grad_normed * normed, -1, keepdims=True)))
    grads = (contract_rows(first_in, grad_proj_low), lax.optimization_barrier(jnp.sum(grad_proj, 0)), contract_rows(mixed_flat, grad_low), bias_sum, contract_rows(second_in, grad_pre_low), lax.optimization_barrier(jnp.sum(grad_pre, 0)), contract_rows(act, grad_low), bias_sum, lax.optimization_barrier(jnp.sum(grad_first * normed, 0)), lax.optimization_barrier(jnp.sum(grad_first, 0)), lax.optimization_barrier(jnp.sum(grad_second * normed, 0)), lax.optimization_barrier(jnp.sum(grad_second, 0)))
    return (layer_out, grad_input, grads)

def reference(hidden_in, segments, positions, project_weight, project_bias, dense_weight, dense_bias, expand_weight, expand_bias, shrink_weight, shrink_bias, first_gain, first_shift, second_gain, second_shift, cotangent):
    params = (project_weight, project_bias, dense_weight, dense_bias, expand_weight, expand_bias, shrink_weight, shrink_bias, first_gain, first_shift, second_gain, second_shift)

    def step(totals, inputs):
        tokens, seg_row, pos_row, grad_top = inputs
        layer_out, grad_input, grads = one_sequence(params, tokens, seg_row, pos_row, grad_top)
        return (tuple((left + right for left, right in zip(totals, grads))), (layer_out, grad_input))
    zeros = tuple((jnp.zeros(param.shape, jnp.float32) for param in params))
    totals, outputs = lax.scan(step, zeros, (hidden_in, segments, positions, cotangent))
    return (outputs[0], outputs[1], totals[0], totals[1], totals[2], totals[3], totals[4], totals[5], totals[6], totals[7], totals[8], totals[9], totals[10], totals[11])
```

```python
import functools
import math

import jax
import jax.numpy as jnp
from jax import lax
from jax.experimental import pallas as pl
from jax.experimental.pallas import tpu as pltpu
from jax.sharding import PartitionSpec as P

HEAD_DIM = 64
ROT = 16
EPS = 1e-05
LOW = jnp.bfloat16
F32 = jnp.float32


def contract_rows(left, right):
    return lax.dot_general(left, right, (((0,), (0,)), ((), ())), preferred_element_type=F32)


def contract_cols(left, right):
    return lax.dot_general(left, right, (((1,), (1,)), ((), ())), preferred_element_type=F32)


def matmul(left, right):
    return jnp.dot(left, right, preferred_element_type=F32)


def after(value, *earlier):
    return lax.optimization_barrier((value, *earlier))[0]


def core_count(ways):
    return 2 if ways % 2 == 0 else 1


def shift(value, axis, step):
    ways = lax.axis_size(axis)
    return lax.ppermute(value, axis, [(i, (i + step) % ways) for i in range(ways)])


def swap_cores(value):
    ways = lax.axis_size("dp")
    return lax.ppermute(value, "dp", [(i, i ^ 1) for i in range(ways)])


def next_chip(value, hops=1):
    return shift(value, "dp", core_count(lax.axis_size("dp")) * hops)


def swap_blocks(blocks):
    ways = lax.axis_size("seq")
    me = lax.axis_index("seq")
    own = lax.dynamic_index_in_dim(blocks, me, 0, keepdims=True)
    out = lax.dynamic_update_slice_in_dim(jnp.zeros_like(blocks), own, me, 0)
    for step in range(1, ways):
        sent = lax.dynamic_index_in_dim(blocks, (me + step) % ways, 0, keepdims=True)
        out = lax.dynamic_update_slice_in_dim(
            out, shift(sent, "seq", step), (me - step) % ways, 0
        )
    return out


def gather_seq(value):
    ways = lax.axis_size("seq")
    me = lax.axis_index("seq")
    out = jnp.zeros((ways,) + value.shape, value.dtype)
    for step in range(ways):
        got = value if step == 0 else shift(value, "seq", step)
        out = lax.dynamic_update_slice_in_dim(out, got[None], (me - step) % ways, 0)
    return out.reshape((ways * value.shape[0],) + value.shape[1:])


def sum_seq(partial):
    ways = lax.axis_size("seq")
    me = lax.axis_index("seq")
    blocks = partial.reshape(ways, partial.shape[0] // ways, partial.shape[1])
    total = lax.dynamic_index_in_dim(blocks, me, 0, keepdims=False)
    for step in range(1, ways):
        sent = lax.dynamic_index_in_dim(blocks, (me + step) % ways, 0, keepdims=False)
        total = total + shift(sent.astype(LOW), "seq", step).astype(F32)
    return total


def sum_all(vector):
    total = vector
    for step in range(1, lax.axis_size("seq")):
        total = total + shift(vector, "seq", step)
    ways = lax.axis_size("dp")
    if core_count(ways) == 2:
        total = total + swap_cores(total)
    chips = ways // core_count(ways)
    out = total
    for step in range(1, chips):
        out = out + next_chip(total, step)
    return out


def gather_dp(shard):
    ways = lax.axis_size("dp")
    cores = core_count(ways)
    chips = ways // cores
    me = lax.axis_index("dp")
    chip, core = me // cores, me % cores
    out = jnp.zeros((ways,) + shard.shape, shard.dtype)
    held = shard
    for step in range(chips):
        if step:
            held = next_chip(held)
        base = ((chip - step) % chips) * cores
        out = lax.dynamic_update_slice_in_dim(out, held[None], base + core, 0)
        if cores == 2:
            out = lax.dynamic_update_slice_in_dim(out, swap_cores(held)[None], base + 1 - core, 0)
    return out.reshape((ways * shard.shape[0],) + shard.shape[1:]), held


def sum_dp(make, send_first=None):
    ways = lax.axis_size("dp")
    cores = core_count(ways)
    chips = ways // cores
    me = lax.axis_index("dp")
    chip, core = me // cores, me % cores
    if cores == 2:
        away = make(1 - core).astype(LOW)
        kept = make(core) + swap_cores(away).astype(F32)
    else:
        kept = make(core)
    total = lax.dynamic_index_in_dim(kept, (chip - 1) % chips, 0, keepdims=False)
    for step in range(1, chips):
        mine = lax.dynamic_index_in_dim(kept, (chip - 1 - step) % chips, 0, keepdims=False)
        total = next_chip(total.astype(LOW)).astype(F32) + mine
    return total


def core_columns(value, core):
    ways = lax.axis_size("dp")
    cores = core_count(ways)
    split = value.reshape(value.shape[0], ways // cores, cores, value.shape[1] // ways)
    return lax.dynamic_index_in_dim(split, core, 2, keepdims=False).reshape(value.shape[0], -1)


def weight_grad(left, right):
    ways = lax.axis_size("dp")
    chips = ways // core_count(ways)

    def make(core):
        return contract_rows(core_columns(left, core), right).reshape(
            chips, left.shape[1] // ways, right.shape[1]
        )

    return sum_dp(make)


def attention_kernel(
    rows, heads, proj_ref, grad_ref, cos_ref, up_ref, down_ref, seg_col_ref, seg_row_ref,
    mixed_ref, out_ref, bias_ref, q_ref, k_ref, v_ref, gq_ref, gk_ref, gv_ref,
):
    length, width = mixed_ref.shape
    half = ROT // 2
    scale = 1.0 / math.sqrt(HEAD_DIM)
    cosine, up, down = cos_ref[...], up_ref[...], down_ref[...]

    def lanes(value, by):
        return pltpu.roll(value, by % width, 1)

    def rotate(value, sign):
        return value * cosine + sign * (lanes(value, -half) * up + lanes(value, half) * down)

    q_ref[...] = rotate(proj_ref[:, :width], 1.0).astype(LOW)
    k_ref[...] = rotate(proj_ref[:, width : 2 * width], 1.0).astype(LOW)
    v_ref[...] = proj_ref[:, 2 * width :].astype(LOW)
    gq_ref[...] = jnp.zeros_like(gq_ref)
    gk_ref[...] = jnp.zeros_like(gk_ref)
    gv_ref[...] = jnp.zeros_like(gv_ref)
    lane = lax.broadcasted_iota(jnp.int32, (1, width), 1)
    for block in range(length // rows):
        here = slice(block * rows, (block + 1) * rows)
        seen = (block + 1) * rows
        row_at = block * rows + lax.broadcasted_iota(jnp.int32, (rows, seen), 0)
        allowed = (lax.broadcasted_iota(jnp.int32, (rows, seen), 1) <= row_at) & (
            seg_row_ref[0:1, :seen] == seg_col_ref[here, :]
        )
        keys, values = k_ref[:seen, :], v_ref[:seen, :]
        query_all, grad_all = q_ref[here, :], grad_ref[here, :]
        mixed_all = jnp.zeros((rows, width), F32)
        for head in range(heads):
            own = (lane >= head * HEAD_DIM) & (lane < (head + 1) * HEAD_DIM)

            def only(value):
                return jnp.where(own, value, jnp.zeros_like(value)) if heads > 1 else value

            query, grad = only(query_all), only(grad_all)
            scores = jnp.where(allowed, contract_cols(query, keys) * scale, -1e30)
            top = jnp.max(scores, -1, keepdims=True)
            weights = jnp.exp(scores - top)
            probs = weights * (1.0 / jnp.sum(weights, -1, keepdims=True))
            probs_low = probs.astype(LOW)
            mixed = matmul(probs_low, only(values)).astype(LOW).astype(F32)
            mixed_all = mixed_all + mixed
            dots = jnp.sum(grad.astype(F32) * mixed, -1, keepdims=True)
            grad_probs = contract_cols(grad, values)
            grad_scores = (probs * (grad_probs - dots) * scale).astype(LOW)
            gq_ref[here, :] += matmul(grad_scores, only(keys))
            gk_ref[:seen, :] += contract_rows(grad_scores, query)
            gv_ref[:seen, :] += contract_rows(probs_low, grad)
        mixed_ref[here, :] = mixed_all.astype(LOW)
    for at, grad in enumerate(
        (rotate(gq_ref[...], -1.0), rotate(gk_ref[...], -1.0), gv_ref[...])
    ):
        out_ref[:, at * width : (at + 1) * width] = grad.astype(LOW)
        bias_ref[:, at * width : (at + 1) * width] = jnp.sum(grad, 0, keepdims=True)


def attention(proj, grad_mixed, tables, segments):
    length, triple = proj.shape
    width = triple // 3
    rows = 256 if length % 256 == 0 else length
    return pl.pallas_call(
        functools.partial(attention_kernel, rows, width // HEAD_DIM),
        out_shape=(
            jax.ShapeDtypeStruct((length, width), LOW),
            jax.ShapeDtypeStruct((length, triple), LOW),
            jax.ShapeDtypeStruct((1, triple), F32),
        ),
        in_specs=[pl.BlockSpec(memory_space=pltpu.VMEM)] * 7,
        out_specs=(pl.BlockSpec(memory_space=pltpu.VMEM),) * 3,
        scratch_shapes=[pltpu.VMEM((length, width), LOW)] * 3
        + [pltpu.VMEM((length, width), F32)] * 3,
        cost_estimate=pl.CostEstimate(
            flops=14 * length * length * width,
            bytes_accessed=12 * length * triple,
            transcendentals=length * length * width // HEAD_DIM,
        ),
        name="attention",
    )(proj, grad_mixed, *tables, segments[:, None], segments[None, :])


def rotary_tables(positions, width):
    half = ROT // 2
    lane = jnp.arange(width) % HEAD_DIM
    inverse = jnp.exp((lane % half).astype(F32) * (-2.0 * math.log(10000.0) / ROT))
    angles = positions.astype(F32)[:, None] * inverse[None, :]
    sine = jnp.sin(angles)
    return (
        jnp.where(lane < ROT, jnp.cos(angles), 1.0),
        jnp.where(lane < half, -sine, 0.0),
        jnp.where((lane >= half) & (lane < ROT), sine, 0.0),
    )


def per_device(
    hidden_in, segments, positions, project_weight, project_bias, dense_weight, dense_bias,
    expand_weight, expand_bias, shrink_weight, shrink_bias, first_gain, first_shift,
    second_gain, second_shift, cotangent,
):
    ways, parts = lax.axis_size("dp"), lax.axis_size("seq")
    dp, seq = lax.axis_index("dp"), lax.axis_index("seq")
    device = dp * parts + seq
    tokens, grad_top = hidden_in[0], cotangent[0]
    count, dim = tokens.shape
    slim = project_weight.shape[0]
    width = dim // parts
    hidden = expand_weight.shape[1] // (ways * parts)
    rows = slim * parts

    vectors = (
        project_bias, dense_bias, expand_bias, shrink_bias,
        first_gain, first_shift, second_gain, second_shift,
    )
    sizes = [vector.shape[0] for vector in vectors]
    placed = [
        lax.dynamic_update_slice_in_dim(
            jnp.zeros((vector.shape[0] * ways * parts,), F32), vector.astype(F32),
            device * vector.shape[0], 0,
        )
        for vector in vectors
    ]
    small = sum_all(jnp.concatenate(placed))
    ends = [0]
    for size in sizes:
        ends.append(ends[-1] + size * ways * parts)
    full = [small[ends[i] : ends[i + 1]] for i in range(len(sizes))]
    project_shift = lax.dynamic_index_in_dim(
        full[0].reshape(3, parts, width), seq, 1, keepdims=False
    ).reshape(1, 3 * width)
    dense_shift, shrink_shift = full[1], full[3]
    expand_shift = lax.dynamic_index_in_dim(
        full[2].reshape(ways, parts, hidden), seq, 1, keepdims=False
    ).reshape(1, ways * hidden)
    gain_one, shift_one, gain_two, shift_two = full[4:]

    centre = jnp.mean(tokens, axis=-1, keepdims=True)
    centred = tokens - centre
    inv_std = lax.rsqrt(jnp.mean(centred * centred, axis=-1, keepdims=True) + EPS)
    normed = centred * inv_std
    normed_all = gather_seq(normed.astype(LOW))
    grad_low = gather_seq(grad_top.astype(LOW))
    places = gather_seq(jnp.stack([segments[0], positions[0]])[None])
    segs = places[:, 0].reshape(-1)
    tables = rotary_tables(places[:, 1].reshape(-1), width)

    project_part = swap_blocks(
        project_weight.reshape(slim, 3, parts, width).transpose(2, 0, 1, 3).reshape(
            parts, slim, 3 * width
        )
    ).reshape(rows, 3 * width)
    expand_part = swap_blocks(
        expand_weight.reshape(slim, ways, parts, hidden).transpose(2, 0, 1, 3).reshape(
            parts, slim, ways * hidden
        )
    ).reshape(rows, ways * hidden)
    shrink, end_shrink = gather_dp(shrink_weight)
    expand, end_expand = gather_dp(expand_part)
    attn_part = jnp.concatenate([project_part, dense_weight.reshape(rows, width)], 1)
    attn_full, unused = gather_dp(after(attn_part, end_shrink))
    project = attn_full[:, : 3 * width]
    dense = swap_blocks(
        attn_full[:, 3 * width :].reshape(parts, (ways // parts) * slim, dim)
    )
    dense = dense.reshape(parts, ways // parts, slim, dim).transpose(1, 0, 2, 3).reshape(width, dim)

    wide = normed_all.astype(F32)
    second_in = (wide * gain_two + shift_two).astype(LOW)
    pre = matmul(second_in, expand) + expand_shift
    cdf = 0.5 * (1.0 + lax.erf(pre * (1.0 / math.sqrt(2.0))))
    act = (pre * cdf).astype(LOW)
    slope = cdf + pre * jnp.exp(-0.5 * pre * pre) * (1.0 / math.sqrt(2.0 * math.pi))
    grad_pre = contract_cols(grad_low, shrink) * slope
    grad_pre_low = grad_pre.astype(LOW)
    shrink_grad = weight_grad(act, grad_low)
    expand_grad = weight_grad(second_in, grad_pre_low)
    expand_grad = swap_blocks(expand_grad.astype(LOW).reshape(parts, slim, ways * hidden))
    expand_grad = (
        expand_grad.reshape(parts, slim, ways, hidden).transpose(1, 2, 0, 3)
        .reshape(slim, ways * parts * hidden).astype(F32)
    )
    mlp_out = matmul(act, shrink)
    grad_second = contract_cols(grad_pre_low, expand)

    first_in = (wide * gain_one + shift_one).astype(LOW)
    proj = matmul(first_in, project) + project_shift
    grad_mixed = contract_cols(grad_low, dense).astype(LOW)
    mixed, grad_proj, grad_bias = attention(proj, grad_mixed, tables, segs)
    attn_out = matmul(mixed, dense)
    layer_out = tokens + dense_shift + shrink_shift + sum_seq(attn_out + mlp_out)
    project_grad = weight_grad(first_in, grad_proj)
    project_grad = swap_blocks(project_grad.astype(LOW).reshape(parts, slim, 3 * width))
    project_grad = (
        project_grad.reshape(parts, slim, 3, width).transpose(1, 2, 0, 3)
        .reshape(slim, 3 * dim).astype(F32)
    )
    dense_rows = contract_rows(mixed, grad_low).astype(LOW)
    dense_rows = swap_blocks(
        dense_rows.reshape(ways // parts, parts, slim, dim).transpose(1, 0, 2, 3)
        .reshape(parts, (ways // parts) * slim, dim)
    )
    cores = core_count(ways)
    dense_blocks = dense_rows.reshape(ways // cores, cores, slim, dim)
    dense_grad = sum_dp(
        lambda core: lax.dynamic_index_in_dim(dense_blocks, core, 1, keepdims=False).astype(F32)
    )
    grad_first = contract_cols(grad_proj, project)

    grad_normed = sum_seq(grad_first * gain_one + grad_second * gain_two)
    grad_input = grad_top + inv_std * (
        grad_normed
        - jnp.mean(grad_normed, -1, keepdims=True)
        - normed * jnp.mean(grad_normed * normed, -1, keepdims=True)
    )

    bias_sum = jnp.sum(grad_top, 0)
    own_bias = lax.dynamic_update_slice_in_dim(
        jnp.zeros((3, parts, width), F32), grad_bias.reshape(3, 1, width), seq, 1
    )
    own_hidden = lax.dynamic_update_slice_in_dim(
        jnp.zeros((ways, parts, hidden), F32),
        jnp.sum(grad_pre, 0).reshape(ways, 1, hidden), seq, 1,
    )
    sums = sum_all(
        jnp.concatenate(
            [
                own_bias.reshape(-1), bias_sum, own_hidden.reshape(-1),
                jnp.sum(grad_first * wide, 0), jnp.sum(grad_first, 0),
                jnp.sum(grad_second * wide, 0), jnp.sum(grad_second, 0),
            ]
        )
    )
    order = (0, 1, 2, 4, 5, 6, 7)
    shares, start = {}, 0
    for which in order:
        shares[which] = lax.dynamic_slice_in_dim(
            sums, start + device * sizes[which], sizes[which], 0
        )
        start += sizes[which] * ways * parts
    return (
        layer_out[None], grad_input[None], project_grad, shares[0], dense_grad, shares[1],
        expand_grad, shares[2], shrink_grad, shares[1],
        shares[4], shares[5], shares[6], shares[7],
    )


def solution(mesh):
    both = ("dp", "seq")
    rows, vector = P(both, None), P(both)
    tokens, places = P("dp", "seq", None), P("dp", "seq")
    return jax.shard_map(
        per_device,
        mesh=mesh,
        in_specs=(
            tokens, places, places, rows, vector, rows, vector, rows, vector, rows, vector,
            vector, vector, vector, vector, tokens,
        ),
        out_specs=(
            tokens, tokens, rows, vector, rows, vector, rows, vector, rows, vector,
            vector, vector, vector, vector,
        ),
        check_vma=False,
    )
```
